32 devices in a mesh: rep: 4 (over y, x), fsdp: 8 (over z, core).
Axes of the slice: x: 2, y: 2, z: 4, core: 2. Of those that a mesh axis runs over, the one named last changes fastest.
Arguments:
- tokens: float32 [4096, 1024], P(('rep', 'fsdp')), may hold values from -6 to 6
- segment_ids: int32 [4096], replicated, may hold values from 0 to 7, never falling along the last dimension, each value on 1 to 1024 neighbouring positions
- cotangent: float32 [4096, 1024], P(('rep', 'fsdp')), may hold values from -6 to 6
- w_qkv: bfloat16 [1024, 2048], P('fsdp'), may hold values from -0.1875 to 0.1875
- w_out: bfloat16 [1024, 1024], P('fsdp'), may hold values from -0.75 to 0.75
- w_gate_up: bfloat16 [1024, 9216], P('fsdp'), may hold values from -0.1875 to 0.1875
- w_down: bfloat16 [4608, 1024], P('fsdp'), may hold values from -0.09375 to 0.09375
- g_attn: bfloat16 [1024], P('fsdp'), may hold values from 0.099609375 to 1.8984375
- g_query: bfloat16 [64], P('fsdp'), may hold values from 0.099609375 to 1.8984375
- g_key: bfloat16 [64], P('fsdp'), may hold values from 0.099609375 to 1.8984375
- g_ffn: bfloat16 [1024], P('fsdp'), may hold values from 0.099609375 to 1.8984375
Outputs:
- output: float32 [4096, 1024], P(('rep', 'fsdp'))
- grad_tokens: float32 [4096, 1024], P(('rep', 'fsdp'))
- grad_w_qkv: float32 [1024, 2048], P('fsdp')
- grad_w_out: float32 [1024, 1024], P('fsdp')
- grad_w_gate_up: float32 [1024, 9216], P('fsdp')
- grad_w_down: float32 [4608, 1024], P('fsdp')
- grad_g_attn: float32 [1024], P('fsdp')
- grad_g_query: float32 [64], P('fsdp')
- grad_g_key: float32 [64], P('fsdp')
- grad_g_ffn: float32 [1024], P('fsdp')
The draws below stay inside these ranges and needn't reach their ends.
Inputs may be any that keep to these rules, and one draw needn't show every extreme that they name: `segment_ids`: segment numbers never fall along the tokens; a segment holds 1 to 1024 tokens and one holds exactly 1024.
All inputs are finite; a program needn't handle non-finite values.
Results may differ from the reference program's by a relative error of at most 0.024.
Values may be sent and summed in bfloat16 or wider, within the bound.
A program may use at most 192 MiB of HBM per device.

```python
import math
import jax
import jax.numpy as jnp
import numpy as np
from jax import lax

D = 1024
QUERY_HEADS = 16
KEY_VALUE_HEADS = 8
HEAD_SIZE = 64
FF = 4608
TOK_DEV = 128
SEQUENCE_TOKENS = 1024
QKVW = 2048
TOKENS = 4096
N_FSDP = 8


def block_scale(own_key, dims, cuts, least, high):
    gain = 1.0
    for position, parts in cuts:
        heights = jax.random.uniform(jax.random.fold_in(jax.random.fold_in(own_key, 6), position), (parts,), jnp.float32, least / len(cuts), high / len(cuts))
        gain = gain * jnp.repeat(jnp.exp(heights), dims[position] // parts).reshape((-1,) + (1,) * (len(dims) - 1 - position))
    return gain


def split_up(number_of, total, bound, slope):
    loads = [(1 << 20) // math.isqrt(standing ** slope) + 1 for standing in range(2, number_of + 1)]
    spare, holding = total - bound - (number_of - 1), [1] * (number_of - 1)
    while spare > 0:
        movable = [i for i in range(number_of - 1) if holding[i] < bound]
        whole, budget = sum([loads[i] for i in movable]), spare
        for i in movable:
            extra = min(bound - holding[i], max(1, budget * loads[i] // whole), spare)
            holding[i] = holding[i] + extra
            spare = spare - extra
    return np.array([bound] + holding)


def uneven(own_key, count, total, bound, slope):
    if count == 2:
        one = jax.random.randint(own_key, (), max(1, total - bound), min(bound, total - 1) + 1)
        return jnp.stack([one, total - one])
    sizes = jnp.asarray(split_up(count, total, bound, slope), jnp.int32)
    couples = (count - 1) // 2
    source_of, receiver = sizes[1:1 + 2 * couples:2], sizes[2:2 + 2 * couples:2]
    slack = jnp.minimum(source_of - 1, bound - receiver)
    shifted = jax.random.randint(jax.random.fold_in(own_key, 1), (couples,), 0, 1 << 20) % (slack + 1)
    sizes = sizes.at[1:1 + 2 * couples:2].set(source_of - shifted).at[2:2 + 2 * couples:2].set(receiver + shifted)
    return sizes[jax.random.permutation(jax.random.fold_in(own_key, 2), count)]


def centred(rng, extent, spread, limit, split=(), kind=jnp.bfloat16):
    entries = jax.random.normal(rng, extent, jnp.float32) * spread
    if len(split) > 0:
        entries = block_scale(rng, extent, split, -0.22, 0.18) * entries
    return jnp.clip(entries, min=-limit, max=limit).astype(kind)


def setup_inputs(seed: int = 0) -> dict:
    splits = jax.random.split(jax.random.key(seed), 12)
    tokens = centred(splits[0], (TOKENS, D), 1.0, 6.0, ((0, 32),), jnp.float32)
    segment_ids = jnp.searchsorted(jnp.cumsum(uneven(splits[1], 2 * TOKENS // SEQUENCE_TOKENS, TOKENS, SEQUENCE_TOKENS, 0)), jnp.arange(TOKENS), side="right").astype(jnp.int32)
    cotangent = centred(splits[2], (TOKENS, D), 1.0, 6.0, ((0, 32),), jnp.float32)
    w_qkv = centred(splits[3], (D, QKVW), D ** -0.5, 0.1875, ((0, 8),))
    w_out = centred(splits[4], (QUERY_HEADS * HEAD_SIZE, D), (QUERY_HEADS * HEAD_SIZE // 16) ** -0.5, 0.75, ((0, 8),))
    w_gate_up = centred(splits[5], (D, 2 * FF), D ** -0.5, 0.1875, ((0, 8),))
    w_down = centred(splits[6], (FF, D), FF ** -0.5, 0.09375, ((0, 8),))
    g_attn = jnp.clip(1.0 + 0.18 * jax.random.normal(splits[7], (D,), jnp.float32), 0.099609375, 1.8984375).astype(jnp.bfloat16)
    g_query = jnp.clip(1.0 + 0.18 * jax.random.normal(splits[8], (HEAD_SIZE,), jnp.float32), 0.099609375, 1.8984375).astype(jnp.bfloat16)
    g_key = jnp.clip(1.0 + 0.18 * jax.random.normal(splits[9], (HEAD_SIZE,), jnp.float32), 0.099609375, 1.8984375).astype(jnp.bfloat16)
    g_ffn = jnp.clip(1.0 + 0.18 * jax.random.normal(splits[10], (D,), jnp.float32), 0.099609375, 1.8984375).astype(jnp.bfloat16)
    return {"tokens": tokens, "segment_ids": segment_ids, "cotangent": cotangent, "w_qkv": w_qkv, "w_out": w_out, "w_gate_up": w_gate_up, "w_down": w_down, "g_attn": g_attn, "g_query": g_query, "g_key": g_key, "g_ffn": g_ffn}


NORM_EPS = 1e-05
ROPE_BASE = 1000000.0
MASK_FILL = -1e+30

def rms_forward(values, gain_vec):
    inv_rms = lax.rsqrt(lax.optimization_barrier(jnp.mean(values * values, axis=-1, keepdims=True)) + NORM_EPS)
    return (values * inv_rms * gain_vec, inv_rms)

def block_sum(terms):
    width = terms.shape[-1]
    partial_sums = lax.optimization_barrier(jnp.sum(terms.reshape(N_FSDP, -1, width), axis=1))
    rounded = lax.optimization_barrier(partial_sums.astype(jnp.bfloat16))
    return lax.optimization_barrier(jnp.sum(rounded.astype(jnp.float32), axis=0))

def block_product(left_arr, right_arr):
    left_blocks = left_arr.astype(jnp.float32).reshape(N_FSDP, TOK_DEV, -1)
    right_blocks = right_arr.astype(jnp.float32).reshape(N_FSDP, TOK_DEV, -1)
    partial_sums = jnp.einsum('ntc,ntd->ncd', left_blocks, right_blocks)
    rounded = lax.optimization_barrier(partial_sums.astype(jnp.bfloat16))
    return lax.optimization_barrier(jnp.sum(rounded.astype(jnp.float32), axis=0))

def root_mean_square_reverse(values, inv_rms, gain_vec, grad_out):
    weighted = grad_out * gain_vec
    grad_values = inv_rms * weighted - values * inv_rms ** 3 * lax.optimization_barrier(jnp.mean(weighted * values, axis=-1, keepdims=True))
    grad_gain = block_sum(grad_out * values * inv_rms)
    return (grad_values, grad_gain)

def rope_tables(positions, head_width):
    half_width = head_width // 2
    freqs_base = ROPE_BASE ** (-2.0 * jnp.arange(half_width, dtype=jnp.float32) / head_width)
    angles = positions.astype(jnp.float32)[:, None] * freqs_base[None, :]
    return (jnp.cos(angles)[:, None, :], jnp.sin(angles)[:, None, :])

def rotary_embed_apply(values, rotary_cosine, rotary_sine):
    half_width = values.shape[-1] // 2
    first_half = values[..., :half_width]
    second_half = values[..., half_width:]
    return jnp.concatenate([first_half * rotary_cosine - second_half * rotary_sine, second_half * rotary_cosine + first_half * rotary_sine], axis=-1)

def rotary_embed_invert(grad_out, rotary_cosine, rotary_sine):
    half_width = grad_out.shape[-1] // 2
    first_half = grad_out[..., :half_width]
    second_half = grad_out[..., half_width:]
    return jnp.concatenate([first_half * rotary_cosine + second_half * rotary_sine, second_half * rotary_cosine - first_half * rotary_sine], axis=-1)

def score_block(query_lowprec, key_lowprec, attention_mask_matrix):
    scale_dot = query_lowprec.shape[-1] ** (-0.5)
    scores = jnp.einsum('qkgd,tkd->kgqt', query_lowprec.astype(jnp.float32), key_lowprec.astype(jnp.float32)) * scale_dot
    return jnp.where(attention_mask_matrix, scores, MASK_FILL)

def attend_forward(query_lowprec, key_lowprec, value_lowprec, attention_mask_matrix):
    scores = score_block(query_lowprec, key_lowprec, attention_mask_matrix)
    top_score = lax.optimization_barrier(jnp.max(scores, axis=-1, keepdims=True))
    expo_terms = jnp.where(attention_mask_matrix, jnp.exp(scores - top_score), 0.0)
    row_total = lax.optimization_barrier(jnp.sum(expo_terms, axis=-1, keepdims=True))
    probs = (expo_terms / row_total).astype(jnp.bfloat16)
    mixed = jnp.einsum('kgqt,tkd->qkgd', probs.astype(jnp.float32), value_lowprec.astype(jnp.float32))
    return (mixed.astype(jnp.bfloat16), top_score + jnp.log(row_total))

def attention_reverse_pass(query_lowprec, key_lowprec, value_lowprec, attention_mask_matrix, attention_lowprec, log_partition_sum, grad_attn):
    scale_dot = query_lowprec.shape[-1] ** (-0.5)
    scores = score_block(query_lowprec, key_lowprec, attention_mask_matrix)
    probs_again = jnp.where(attention_mask_matrix, jnp.exp(scores - log_partition_sum), 0.0)
    probs_low = probs_again.astype(jnp.bfloat16).astype(jnp.float32)
    grad_float = grad_attn.astype(jnp.float32)
    value_gradient_rows = jnp.einsum('kgqt,qkgd->tkd', probs_low, grad_float)
    d_probs = jnp.einsum('qkgd,tkd->kgqt', grad_float, value_lowprec.astype(jnp.float32))
    delta_rows = lax.optimization_barrier(jnp.sum(grad_float * attention_lowprec.astype(jnp.float32), axis=-1))
    delta_rows = jnp.transpose(delta_rows, (1, 2, 0))[..., None]
    d_score = (probs_again * (d_probs - delta_rows) * scale_dot).astype(jnp.bfloat16).astype(jnp.float32)
    grad_query = jnp.einsum('kgqt,tkd->qkgd', d_score, key_lowprec.astype(jnp.float32))
    grad_key = jnp.einsum('kgqt,qkgd->tkd', d_score, query_lowprec.astype(jnp.float32))
    return (grad_query, grad_key, value_gradient_rows)

def reference(tokens, segment_ids, cotangent, w_qkv, w_out, w_gate_up, w_down, g_attn, g_query, g_key, g_ffn):
    seq_count = TOKENS // SEQUENCE_TOKENS
    cluster_size = QUERY_HEADS // KEY_VALUE_HEADS
    gain_sequence = [gain_arr.astype(jnp.float32) for gain_arr in (g_attn, g_query, g_key, g_ffn)]
    positions = jnp.arange(SEQUENCE_TOKENS, dtype=jnp.int32)
    rotary_cosine, rotary_sine = rope_tables(positions, HEAD_SIZE)
    causal = positions[None, :] <= positions[:, None]

    def one_sequence(totals, inputs_now):
        seq_tokens, seq_segments, seq_cot = inputs_now
        attention_mask_matrix = causal & (seq_segments[:, None] == seq_segments[None, :])
        normed_f, inv_in = rms_forward(seq_tokens, gain_sequence[0])
        normed_in = normed_f.astype(jnp.bfloat16)
        projection_output = jnp.dot(normed_in, w_qkv, preferred_element_type=jnp.float32)
        query_raw = projection_output[:, :QUERY_HEADS * HEAD_SIZE].reshape(SEQUENCE_TOKENS, QUERY_HEADS, HEAD_SIZE)
        key_unrotated = projection_output[:, QUERY_HEADS * HEAD_SIZE:(QUERY_HEADS + KEY_VALUE_HEADS) * HEAD_SIZE].reshape(SEQUENCE_TOKENS, KEY_VALUE_HEADS, HEAD_SIZE)
        value_lowprec = projection_output[:, (QUERY_HEADS + KEY_VALUE_HEADS) * HEAD_SIZE:].reshape(SEQUENCE_TOKENS, KEY_VALUE_HEADS, HEAD_SIZE).astype(jnp.bfloat16)
        query_norm_output, inv_query = rms_forward(query_raw, gain_sequence[1])
        key_norm, key_inverse_norm = rms_forward(key_unrotated, gain_sequence[2])
        query_lowprec = rotary_embed_apply(query_norm_output, rotary_cosine, rotary_sine).astype(jnp.bfloat16).reshape(SEQUENCE_TOKENS, KEY_VALUE_HEADS, cluster_size, HEAD_SIZE)
        key_lowprec = rotary_embed_apply(key_norm, rotary_cosine, rotary_sine).astype(jnp.bfloat16)
        attention_lowprec, log_partition_sum = attend_forward(query_lowprec, key_lowprec, value_lowprec, attention_mask_matrix)
        attn_flat = attention_lowprec.reshape(SEQUENCE_TOKENS, QUERY_HEADS * HEAD_SIZE)
        mid_stream = seq_tokens + jnp.dot(attn_flat, w_out, preferred_element_type=jnp.float32)
        normed_g, inv_mid = rms_forward(mid_stream, gain_sequence[3])
        normed_mid = normed_g.astype(jnp.bfloat16)
        gate_up = jnp.dot(normed_mid, w_gate_up, preferred_element_type=jnp.float32)
        gate_part = gate_up[:, :FF]
        up_part = gate_up[:, FF:]
        sigmoid_gate = jax.nn.sigmoid(gate_part)
        hidden = (gate_part * sigmoid_gate * up_part).astype(jnp.bfloat16)
        seq_out = mid_stream + jnp.dot(hidden, w_down, preferred_element_type=jnp.float32)
        cot_low = seq_cot.astype(jnp.bfloat16)
        grad_down = block_product(hidden, cot_low)
        d_hidden = jnp.dot(cot_low, w_down.T, preferred_element_type=jnp.float32)
        d_gate = d_hidden * up_part * sigmoid_gate * (1.0 + gate_part * (1.0 - sigmoid_gate))
        d_up = d_hidden * gate_part * sigmoid_gate
        d_gate_up = jnp.concatenate([d_gate, d_up], axis=1).astype(jnp.bfloat16)
        grad_gate_up = block_product(normed_mid, d_gate_up)
        d_normed_mid = jnp.dot(d_gate_up, w_gate_up.T, preferred_element_type=jnp.float32)
        back_mid, grad_ffn_gain = root_mean_square_reverse(mid_stream, inv_mid, gain_sequence[3], d_normed_mid)
        d_mid = seq_cot + back_mid
        middle_cotangent_lowprec = d_mid.astype(jnp.bfloat16)
        grad_out_proj = block_product(attn_flat, middle_cotangent_lowprec)
        attention_cotangent = jnp.dot(middle_cotangent_lowprec, w_out.T, preferred_element_type=jnp.float32).astype(jnp.bfloat16)
        attention_cotangent = attention_cotangent.reshape(SEQUENCE_TOKENS, KEY_VALUE_HEADS, cluster_size, HEAD_SIZE)
        query_lowprec_gradient, key_lowprec_gradient, value_gradient_rows = attention_reverse_pass(query_lowprec, key_lowprec, value_lowprec, attention_mask_matrix, attention_lowprec, log_partition_sum, attention_cotangent)
        d_query, grad_query_gain = root_mean_square_reverse(query_raw, inv_query, gain_sequence[1], rotary_embed_invert(query_lowprec_gradient.reshape(SEQUENCE_TOKENS, QUERY_HEADS, HEAD_SIZE), rotary_cosine, rotary_sine))
        key_cotangent, key_gain_gradient = root_mean_square_reverse(key_unrotated, key_inverse_norm, gain_sequence[2], rotary_embed_invert(key_lowprec_gradient, rotary_cosine, rotary_sine))
        d_projected = jnp.concatenate([d_query.reshape(SEQUENCE_TOKENS, -1), key_cotangent.reshape(SEQUENCE_TOKENS, -1), value_gradient_rows.reshape(SEQUENCE_TOKENS, -1)], axis=1).astype(jnp.bfloat16)
        grad_qkv = block_product(normed_in, d_projected)
        d_normed_in = jnp.dot(d_projected, w_qkv.T, preferred_element_type=jnp.float32)
        back_in, grad_attn_gain = root_mean_square_reverse(seq_tokens, inv_in, gain_sequence[0], d_normed_in)
        grads_now = (grad_qkv, grad_out_proj, grad_gate_up, grad_down, grad_attn_gain, grad_query_gain, key_gain_gradient, grad_ffn_gain)
        totals = tuple((total_now + grad_now for total_now, grad_now in zip(totals, grads_now)))
        return (totals, (seq_out, d_mid + back_in))
    zeros_init = (jnp.zeros((D, QKVW), jnp.float32), jnp.zeros((QUERY_HEADS * HEAD_SIZE, D), jnp.float32), jnp.zeros((D, 2 * FF), jnp.float32), jnp.zeros((FF, D), jnp.float32), jnp.zeros((D,), jnp.float32), jnp.zeros((HEAD_SIZE,), jnp.float32), jnp.zeros((HEAD_SIZE,), jnp.float32), jnp.zeros((D,), jnp.float32))
    stacked_inputs = (tokens.reshape(seq_count, SEQUENCE_TOKENS, D), segment_ids.reshape(seq_count, SEQUENCE_TOKENS), cotangent.reshape(seq_count, SEQUENCE_TOKENS, D))
    totals, outputs_all = lax.scan(one_sequence, zeros_init, stacked_inputs)
    output = outputs_all[0].reshape(TOKENS, D)
    grad_tokens = outputs_all[1].reshape(TOKENS, D)
    return (output, grad_tokens, totals[0], totals[1], totals[2], totals[3], totals[4], totals[5], totals[6], totals[7])
```

```python
import jax
import jax.numpy as jnp
from jax import lax
from jax.sharding import PartitionSpec as P

QUERY_HEADS = 16
KEY_VALUE_HEADS = 8
HEAD_SIZE = 64
FF = 4608


NORM_EPS = 1e-05
ROPE_BASE = 1000000.0
MASK_FILL = -1e30


def rms_forward(values, gain_vec):
    inv_rms = lax.rsqrt(jnp.mean(values * values, axis=-1, keepdims=True) + NORM_EPS)
    return (values * inv_rms * gain_vec, inv_rms)


def root_mean_square_reverse(values, inv_rms, gain_vec, grad_out):
    weighted = grad_out * gain_vec
    grad_values = inv_rms * weighted - values * inv_rms**3 * jnp.mean(
        weighted * values, axis=-1, keepdims=True
    )
    grad_gain = jnp.sum((grad_out * values * inv_rms).reshape(-1, values.shape[-1]), axis=0)
    return (grad_values, grad_gain)


def rope_tables(positions, head_width):
    half_width = head_width // 2
    freqs_base = ROPE_BASE ** (-2.0 * jnp.arange(half_width, dtype=jnp.float32) / head_width)
    angles = positions.astype(jnp.float32)[:, None] * freqs_base[None, :]
    return (jnp.cos(angles)[:, None, :], jnp.sin(angles)[:, None, :])


def rotary_embed_apply(values, rotary_cosine, rotary_sine):
    half_width = values.shape[-1] // 2
    first_half = values[..., :half_width]
    second_half = values[..., half_width:]
    return jnp.concatenate(
        [
            first_half * rotary_cosine - second_half * rotary_sine,
            second_half * rotary_cosine + first_half * rotary_sine,
        ],
        axis=-1,
    )


def rotary_embed_invert(grad_out, rotary_cosine, rotary_sine):
    half_width = grad_out.shape[-1] // 2
    first_half = grad_out[..., :half_width]
    second_half = grad_out[..., half_width:]
    return jnp.concatenate(
        [
            first_half * rotary_cosine + second_half * rotary_sine,
            second_half * rotary_cosine - first_half * rotary_sine,
        ],
        axis=-1,
    )


def score_block(query_lowprec, key_lowprec, attention_mask_matrix):
    scale_dot = query_lowprec.shape[-1] ** (-0.5)
    scores = (
        jnp.einsum("qkgd,tkd->kgqt", query_lowprec, key_lowprec, preferred_element_type=jnp.float32)
        * scale_dot
    )
    return jnp.where(attention_mask_matrix, scores, MASK_FILL)


def attend_forward(query_lowprec, key_lowprec, value_lowprec, attention_mask_matrix):
    scores = score_block(query_lowprec, key_lowprec, attention_mask_matrix)
    top_score = jnp.max(scores, axis=-1, keepdims=True)
    expo_terms = jnp.where(attention_mask_matrix, jnp.exp(scores - top_score), 0.0)
    row_total = jnp.sum(expo_terms, axis=-1, keepdims=True)
    probs = (expo_terms / row_total).astype(jnp.bfloat16)
    mixed = jnp.einsum("kgqt,tkd->qkgd", probs, value_lowprec, preferred_element_type=jnp.float32)
    return (mixed.astype(jnp.bfloat16), top_score + jnp.log(row_total))


def attention_reverse_pass(
    query_lowprec,
    key_lowprec,
    value_lowprec,
    attention_mask_matrix,
    attention_lowprec,
    log_partition_sum,
    grad_attn,
):
    scale_dot = query_lowprec.shape[-1] ** (-0.5)
    scores = score_block(query_lowprec, key_lowprec, attention_mask_matrix)
    probs_again = jnp.where(attention_mask_matrix, jnp.exp(scores - log_partition_sum), 0.0)
    probs_low = probs_again.astype(jnp.bfloat16)
    value_gradient_rows = jnp.einsum(
        "kgqt,qkgd->tkd", probs_low, grad_attn, preferred_element_type=jnp.float32
    )
    d_probs = jnp.einsum(
        "qkgd,tkd->kgqt", grad_attn, value_lowprec, preferred_element_type=jnp.float32
    )
    delta_rows = jnp.sum(
        grad_attn.astype(jnp.float32) * attention_lowprec.astype(jnp.float32), axis=-1
    )
    delta_rows = jnp.transpose(delta_rows, (1, 2, 0))[..., None]
    d_score = (probs_again * (d_probs - delta_rows) * scale_dot).astype(jnp.bfloat16)
    grad_query = jnp.einsum(
        "kgqt,tkd->qkgd", d_score, key_lowprec, preferred_element_type=jnp.float32
    )
    grad_key = jnp.einsum(
        "kgqt,qkgd->tkd", d_score, query_lowprec, preferred_element_type=jnp.float32
    )
    return (grad_query, grad_key, value_gradient_rows)


def tdot(left_arr, right_arr):
    return lax.dot_general(
        left_arr, right_arr, (((0,), (0,)), ((), ())), preferred_element_type=jnp.float32
    )


def transposed_product(left_arr, right_arr):
    return lax.dot_general(
        left_arr, right_arr, (((1,), (1,)), ((), ())), preferred_element_type=jnp.float32
    )


def gathered_weights_body(
    tokens, segment_ids, cotangent, w_qkv, w_out, w_gate_up, w_down, g_attn, g_query, g_key, g_ffn
):
    local_rows = tokens.shape[0]
    cluster_size = QUERY_HEADS // KEY_VALUE_HEADS
    seq_devices = lax.axis_size("fsdp")
    cluster_rows = seq_devices * local_rows
    member = lax.axis_index("fsdp")
    own_group = member * local_rows
    group_start = lax.axis_index("rep") * cluster_rows
    own_global = group_start + own_group
    key_value_width = KEY_VALUE_HEADS * HEAD_SIZE
    shards = (w_qkv, w_out, w_gate_up, w_down, g_attn, g_query, g_key, g_ffn)
    collected_rows = (
        lax.all_gather(shards[0], "fsdp", axis=0, tiled=True),
        lax.all_gather(shards[1], "fsdp", axis=0, tiled=True),
        lax.all_gather(shards[2], "fsdp", axis=0, tiled=True),
        lax.all_gather(shards[3], "fsdp", axis=0, tiled=True),
        lax.all_gather(shards[4], "fsdp", axis=0, tiled=True),
        lax.all_gather(shards[5], "fsdp", axis=0, tiled=True),
        lax.all_gather(shards[6], "fsdp", axis=0, tiled=True),
        lax.all_gather(shards[7], "fsdp", axis=0, tiled=True),
    )
    gain_sequence = [gain_arr.astype(jnp.float32) for gain_arr in collected_rows[4:]]
    query_seg = lax.dynamic_slice_in_dim(segment_ids, own_global, local_rows)
    key_seg = lax.dynamic_slice_in_dim(segment_ids, group_start, cluster_rows)
    query_pos = own_group + jnp.arange(local_rows, dtype=jnp.int32)
    key_pos = jnp.arange(cluster_rows, dtype=jnp.int32)
    attention_mask_matrix = (key_pos[None, :] <= query_pos[:, None]) & (
        query_seg[:, None] == key_seg[None, :]
    )
    rotary_cosine, rotary_sine = rope_tables(query_pos, HEAD_SIZE)
    normed_f, inv_in = rms_forward(tokens, gain_sequence[0])
    normed_in = normed_f.astype(jnp.bfloat16)
    projection_output = jnp.dot(normed_in, collected_rows[0], preferred_element_type=jnp.float32)
    query_raw = projection_output[:, : QUERY_HEADS * HEAD_SIZE].reshape(
        local_rows, QUERY_HEADS, HEAD_SIZE
    )
    key_unrotated = projection_output[
        :, QUERY_HEADS * HEAD_SIZE : (QUERY_HEADS + KEY_VALUE_HEADS) * HEAD_SIZE
    ].reshape(local_rows, KEY_VALUE_HEADS, HEAD_SIZE)
    value_lowprec = projection_output[:, (QUERY_HEADS + KEY_VALUE_HEADS) * HEAD_SIZE :].astype(
        jnp.bfloat16
    )
    query_norm_output, inv_query = rms_forward(query_raw, gain_sequence[1])
    key_norm, key_inverse_norm = rms_forward(key_unrotated, gain_sequence[2])
    query_lowprec = (
        rotary_embed_apply(query_norm_output, rotary_cosine, rotary_sine)
        .astype(jnp.bfloat16)
        .reshape(local_rows, KEY_VALUE_HEADS, cluster_size, HEAD_SIZE)
    )
    key_lowprec = rotary_embed_apply(key_norm, rotary_cosine, rotary_sine).astype(jnp.bfloat16)
    kv_pair = jnp.stack([key_lowprec.reshape(local_rows, key_value_width), value_lowprec])
    key_value_span = lax.all_gather(kv_pair, "fsdp", axis=1, tiled=True)
    span_keys = key_value_span[0].reshape(cluster_rows, KEY_VALUE_HEADS, HEAD_SIZE)
    span_values = key_value_span[1].reshape(cluster_rows, KEY_VALUE_HEADS, HEAD_SIZE)
    attention_lowprec, log_partition_sum = attend_forward(
        query_lowprec, span_keys, span_values, attention_mask_matrix
    )
    attn_flat = attention_lowprec.reshape(local_rows, QUERY_HEADS * HEAD_SIZE)
    mid_stream = tokens + jnp.dot(attn_flat, collected_rows[1], preferred_element_type=jnp.float32)
    normed_g, inv_mid = rms_forward(mid_stream, gain_sequence[3])
    normed_mid = normed_g.astype(jnp.bfloat16)
    gate_up = jnp.dot(normed_mid, collected_rows[2], preferred_element_type=jnp.float32)
    gate_part = gate_up[:, :FF]
    up_part = gate_up[:, FF:]
    sigmoid_gate = jax.nn.sigmoid(gate_part)
    hidden = (gate_part * sigmoid_gate * up_part).astype(jnp.bfloat16)
    output = mid_stream + jnp.dot(hidden, collected_rows[3], preferred_element_type=jnp.float32)
    cot_low = cotangent.astype(jnp.bfloat16)
    grad_down = tdot(hidden, cot_low)
    d_hidden = transposed_product(cot_low, collected_rows[3])
    d_gate = d_hidden * up_part * sigmoid_gate * (1.0 + gate_part * (1.0 - sigmoid_gate))
    d_up = d_hidden * gate_part * sigmoid_gate
    d_gate_up = jnp.concatenate([d_gate, d_up], axis=1).astype(jnp.bfloat16)
    grad_gate_up = tdot(normed_mid, d_gate_up)
    d_normed_mid = transposed_product(d_gate_up, collected_rows[2])
    back_mid, grad_ffn_gain = root_mean_square_reverse(
        mid_stream, inv_mid, gain_sequence[3], d_normed_mid
    )
    d_mid = cotangent + back_mid
    middle_cotangent_lowprec = d_mid.astype(jnp.bfloat16)
    grad_out_proj = tdot(attn_flat, middle_cotangent_lowprec)
    attention_cotangent = (
        transposed_product(middle_cotangent_lowprec, collected_rows[1])
        .astype(jnp.bfloat16)
        .reshape(local_rows, KEY_VALUE_HEADS, cluster_size, HEAD_SIZE)
    )
    query_lowprec_gradient, grad_kwin, grad_vwin = attention_reverse_pass(
        query_lowprec,
        span_keys,
        span_values,
        attention_mask_matrix,
        attention_lowprec,
        log_partition_sum,
        attention_cotangent,
    )
    kv_grads = jnp.stack(
        [
            grad_kwin.reshape(cluster_rows, key_value_width),
            grad_vwin.reshape(cluster_rows, key_value_width),
        ]
    )
    local_key_value = lax.psum_scatter(
        kv_grads.astype(jnp.bfloat16), "fsdp", scatter_dimension=1, tiled=True
    ).astype(jnp.float32)
    d_query, grad_query_gain = root_mean_square_reverse(
        query_raw,
        inv_query,
        gain_sequence[1],
        rotary_embed_invert(
            query_lowprec_gradient.reshape(local_rows, QUERY_HEADS, HEAD_SIZE),
            rotary_cosine,
            rotary_sine,
        ),
    )
    key_cotangent, key_gain_gradient = root_mean_square_reverse(
        key_unrotated,
        key_inverse_norm,
        gain_sequence[2],
        rotary_embed_invert(
            local_key_value[0].reshape(local_rows, KEY_VALUE_HEADS, HEAD_SIZE),
            rotary_cosine,
            rotary_sine,
        ),
    )
    d_projected = jnp.concatenate(
        [
            d_query.reshape(local_rows, -1),
            key_cotangent.reshape(local_rows, -1),
            local_key_value[1],
        ],
        axis=1,
    ).astype(jnp.bfloat16)
    grad_qkv = tdot(normed_in, d_projected)
    d_normed_in = transposed_product(d_projected, collected_rows[0])
    back_in, grad_attn_gain = root_mean_square_reverse(
        tokens, inv_in, gain_sequence[0], d_normed_in
    )
    grad_tokens = d_mid + back_in
    grads_local = (
        grad_qkv,
        grad_out_proj,
        grad_gate_up,
        grad_down,
        grad_attn_gain,
        grad_query_gain,
        key_gain_gradient,
        grad_ffn_gain,
    )
    grad_share = (
        lax.psum_scatter(
            grads_local[0].astype(jnp.bfloat16), "fsdp", scatter_dimension=0, tiled=True
        ).astype(jnp.float32),
        lax.psum_scatter(
            grads_local[1].astype(jnp.bfloat16), "fsdp", scatter_dimension=0, tiled=True
        ).astype(jnp.float32),
        lax.psum_scatter(
            grads_local[2].astype(jnp.bfloat16), "fsdp", scatter_dimension=0, tiled=True
        ).astype(jnp.float32),
        lax.psum_scatter(
            grads_local[3].astype(jnp.bfloat16), "fsdp", scatter_dimension=0, tiled=True
        ).astype(jnp.float32),
        lax.psum_scatter(
            grads_local[4].astype(jnp.bfloat16), "fsdp", scatter_dimension=0, tiled=True
        ).astype(jnp.float32),
        lax.psum_scatter(
            grads_local[5].astype(jnp.bfloat16), "fsdp", scatter_dimension=0, tiled=True
        ).astype(jnp.float32),
        lax.psum_scatter(
            grads_local[6].astype(jnp.bfloat16), "fsdp", scatter_dimension=0, tiled=True
        ).astype(jnp.float32),
        lax.psum_scatter(
            grads_local[7].astype(jnp.bfloat16), "fsdp", scatter_dimension=0, tiled=True
        ).astype(jnp.float32),
    )
    grad_total = (
        lax.psum(grad_share[0].astype(jnp.bfloat16), "rep").astype(jnp.float32),
        lax.psum(grad_share[1].astype(jnp.bfloat16), "rep").astype(jnp.float32),
        lax.psum(grad_share[2].astype(jnp.bfloat16), "rep").astype(jnp.float32),
        lax.psum(grad_share[3].astype(jnp.bfloat16), "rep").astype(jnp.float32),
        lax.psum(grad_share[4].astype(jnp.bfloat16), "rep").astype(jnp.float32),
        lax.psum(grad_share[5].astype(jnp.bfloat16), "rep").astype(jnp.float32),
        lax.psum(grad_share[6].astype(jnp.bfloat16), "rep").astype(jnp.float32),
        lax.psum(grad_share[7].astype(jnp.bfloat16), "rep").astype(jnp.float32),
    )
    return (
        output,
        grad_tokens,
        grad_total[0],
        grad_total[1],
        grad_total[2],
        grad_total[3],
        grad_total[4],
        grad_total[5],
        grad_total[6],
        grad_total[7],
    )


def shift_exchange(parts, axis_name):
    count = parts.shape[0]
    me = lax.axis_index(axis_name)
    result = jnp.zeros_like(parts)
    own = lax.dynamic_index_in_dim(parts, me, 0, keepdims=True)
    result = lax.dynamic_update_slice_in_dim(result, own, me, 0)
    for shift in range(1, count):
        chunk = lax.dynamic_index_in_dim(parts, (me + shift) % count, 0, keepdims=True)
        landed = lax.ppermute(
            chunk, axis_name, [(i, (i + shift) % count) for i in range(count)]
        )
        result = lax.dynamic_update_slice_in_dim(result, landed, (me - shift) % count, 0)
    return result


def shift_reduce_scatter(parts, axis_name):
    count = parts.shape[0]
    me = lax.axis_index(axis_name)
    total = lax.dynamic_index_in_dim(parts, me, 0, keepdims=False).astype(jnp.float32)
    for shift in range(1, count):
        chunk = lax.dynamic_index_in_dim(parts, (me + shift) % count, 0, keepdims=False)
        landed = lax.ppermute(
            chunk, axis_name, [(i, (i + shift) % count) for i in range(count)]
        )
        total = total + landed.astype(jnp.float32)
    return total


def shift_gather(piece, axis_name):
    count = lax.axis_size(axis_name)
    me = lax.axis_index(axis_name)
    result = jnp.zeros((count,) + piece.shape, piece.dtype)
    result = lax.dynamic_update_slice_in_dim(result, piece[None], me, 0)
    for shift in range(1, count):
        landed = lax.ppermute(
            piece[None], axis_name, [(i, (i + shift) % count) for i in range(count)]
        )
        result = lax.dynamic_update_slice_in_dim(result, landed, (me - shift) % count, 0)
    return result


def rep_sum_rows(grad):
    copies = lax.axis_size("rep")
    rows, columns = grad.shape
    parts = grad.astype(jnp.bfloat16).reshape(copies, rows // copies, columns)
    summed = shift_reduce_scatter(parts, "rep").astype(jnp.bfloat16)
    return shift_gather(summed, "rep").reshape(rows, columns).astype(jnp.float32)


def rep_sum_columns(grad, members, extra=None):
    copies = lax.axis_size("rep")
    rows = grad.shape[0] // members
    columns = grad.shape[1]
    parts = grad.astype(jnp.bfloat16).reshape(members, copies, rows // copies, columns)
    if extra is not None:
        rider = jnp.broadcast_to(
            extra.astype(jnp.bfloat16)[:, None], (members, copies) + extra.shape[1:]
        )
        parts = jnp.concatenate([parts, rider], axis=2)
    summed = shift_reduce_scatter(parts.transpose(1, 0, 2, 3), "rep").astype(jnp.bfloat16)
    swapped = shift_exchange(summed, "fsdp")
    if extra is not None:
        extra = jnp.sum(swapped[:, rows // copies :].astype(jnp.float32), axis=0)
        swapped = swapped[:, : rows // copies]
    full = shift_gather(swapped, "rep")
    full = full.transpose(1, 0, 2, 3).reshape(members, rows, columns)
    return full if extra is None else (full, extra)


def split_heads(values, heads):
    return values.reshape(values.shape[0], heads, HEAD_SIZE).transpose(1, 0, 2)


def join_heads(values):
    return values.transpose(1, 0, 2).reshape(values.shape[1], -1)


def rms_inverse(values):
    return lax.rsqrt(jnp.mean(values * values, axis=-1, keepdims=True) + NORM_EPS)


def weighted_norm_reverse(values, inv_rms, weighted):
    return inv_rms * weighted - values * inv_rms**3 * jnp.mean(
        weighted * values, axis=-1, keepdims=True
    )


def rotate(values, cosine, sine):
    half = values.shape[-1] // 2
    first, second = values[..., :half], values[..., half:]
    return jnp.concatenate([first * cosine - second * sine, second * cosine + first * sine], -1)


def split_columns_body(
    tokens, segment_ids, cotangent, w_qkv, w_out, w_gate_up, w_down, g_attn, g_query, g_key, g_ffn
):
    bf16, f32 = jnp.bfloat16, jnp.float32
    local_rows, width = tokens.shape
    members = lax.axis_size("fsdp")
    member = lax.axis_index("fsdp")
    rows = members * local_rows
    shard = w_qkv.shape[0]
    q_heads = QUERY_HEADS // members
    kv_heads = KEY_VALUE_HEADS // members
    group = QUERY_HEADS // KEY_VALUE_HEADS
    q_cols, kv_cols = q_heads * HEAD_SIZE, kv_heads * HEAD_SIZE
    q_all, kv_all = QUERY_HEADS * HEAD_SIZE, KEY_VALUE_HEADS * HEAD_SIZE
    hid = w_down.shape[0]
    g_attn_col = g_attn.astype(f32)[:, None]
    g_ffn_col = g_ffn.astype(f32)[:, None]

    inv_in = rms_inverse(tokens)
    unit_in = lax.all_gather((tokens * inv_in).astype(bf16), "fsdp", axis=0, tiled=True)
    scaled_qkv = (w_qkv.astype(f32) * g_attn_col).astype(bf16)
    qkv_parts = jnp.concatenate(
        [
            scaled_qkv[:, :q_all].reshape(shard, members, q_cols),
            scaled_qkv[:, q_all : q_all + kv_all].reshape(shard, members, kv_cols),
            scaled_qkv[:, q_all + kv_all :].reshape(shard, members, kv_cols),
        ],
        axis=2,
    ).transpose(1, 0, 2)
    qkv_cols = shift_exchange(qkv_parts, "fsdp").reshape(members * shard, q_cols + 2 * kv_cols)
    scaled_gu = (w_gate_up.astype(f32) * g_ffn_col).astype(bf16)
    gu_parts = scaled_gu.reshape(shard, 2, members, hid).transpose(2, 0, 1, 3)
    gu_parts = gu_parts.reshape(members, shard, 2 * hid)
    gu_cols = shift_exchange(gu_parts, "fsdp").reshape(members * shard, 2 * hid)
    gains = lax.all_gather(jnp.stack([g_query, g_key]), "fsdp", axis=1, tiled=True).astype(f32)
    gain_q, gain_k = gains[0], gains[1]
    cot_low = lax.all_gather(cotangent.astype(bf16), "fsdp", axis=0, tiled=True)

    seg = lax.dynamic_slice_in_dim(segment_ids, lax.axis_index("rep") * rows, rows)
    pos = jnp.arange(rows, dtype=jnp.int32)
    mask = ((pos[None, :] <= pos[:, None]) & (seg[:, None] == seg[None, :]))[None, None]
    half = HEAD_SIZE // 2
    freqs = ROPE_BASE ** (-2.0 * jnp.arange(half, dtype=f32) / HEAD_SIZE)
    angles = pos.astype(f32)[:, None] * freqs[None, :]
    cosine, sine = jnp.cos(angles), jnp.sin(angles)
    scale = HEAD_SIZE ** (-0.5)

    projected = jnp.dot(unit_in, qkv_cols, preferred_element_type=f32)
    query = split_heads(projected[:, :q_cols], q_heads)
    key = split_heads(projected[:, q_cols : q_cols + kv_cols], kv_heads)
    value_low = split_heads(projected[:, q_cols + kv_cols :].astype(bf16), kv_heads)
    inv_query, inv_key = rms_inverse(query), rms_inverse(key)
    query_low = rotate(query * inv_query * gain_q, cosine, sine).astype(bf16)
    query_low = query_low.reshape(kv_heads, group, rows, HEAD_SIZE)
    key_low = rotate(key * inv_key * gain_k, cosine, sine).astype(bf16)

    def scores_of():
        raw = jnp.einsum("kgqd,ktd->kgqt", query_low, key_low, preferred_element_type=f32)
        return jnp.where(mask, raw * scale, MASK_FILL)

    scores = scores_of()
    top = jnp.max(scores, axis=-1, keepdims=True)
    expo = jnp.where(mask, jnp.exp(scores - top), 0.0)
    total = jnp.sum(expo, axis=-1, keepdims=True)
    probs = (expo / total).astype(bf16)
    attn = jnp.einsum("kgqt,ktd->kgqd", probs, value_low, preferred_element_type=f32).astype(bf16)
    attn_flat = join_heads(attn.reshape(q_heads, rows, HEAD_SIZE))
    out_part = jnp.dot(attn_flat, w_out, preferred_element_type=f32).astype(bf16)
    mid = tokens + lax.psum_scatter(
        out_part, "fsdp", scatter_dimension=0, tiled=True
    ).astype(f32)

    inv_mid = rms_inverse(mid)
    unit_mid = lax.all_gather((mid * inv_mid).astype(bf16), "fsdp", axis=0, tiled=True)
    w_gate, w_up = gu_cols[:, :hid], gu_cols[:, hid:]
    gate = jnp.dot(unit_mid, w_gate, preferred_element_type=f32)
    up = jnp.dot(unit_mid, w_up, preferred_element_type=f32)
    d_hidden = transposed_product(cot_low, w_down)
    sig = jax.nn.sigmoid(gate)
    hidden = (gate * sig * up).astype(bf16)
    d_gate = (d_hidden * up * sig * (1.0 + gate * (1.0 - sig))).astype(bf16)
    d_up = (d_hidden * gate * sig).astype(bf16)
    d_unit_mid = (transposed_product(d_gate, w_gate) + transposed_product(d_up, w_up)).astype(bf16)
    weighted_mid = lax.psum_scatter(
        d_unit_mid, "fsdp", scatter_dimension=0, tiled=True
    ).astype(f32)
    d_mid = cotangent + weighted_norm_reverse(mid, inv_mid, weighted_mid)
    d_mid_low = lax.all_gather(d_mid.astype(bf16), "fsdp", axis=0, tiled=True)

    hidden_late, _ = lax.optimization_barrier((hidden, weighted_mid))
    down_part = jnp.dot(hidden_late, w_down, preferred_element_type=f32).astype(bf16)
    down_part, _ = lax.optimization_barrier((down_part, d_mid_low))
    output = mid + lax.psum_scatter(
        down_part, "fsdp", scatter_dimension=0, tiled=True
    ).astype(f32)
    grad_gu = jnp.concatenate([tdot(unit_mid, d_gate), tdot(unit_mid, d_up)], axis=1)
    grad_gu = rep_sum_columns(grad_gu, members)
    grad_gu = grad_gu.reshape(members, shard, 2, hid).transpose(1, 2, 0, 3).reshape(shard, -1)
    grad_gu = grad_gu.astype(f32)
    grad_down = rep_sum_rows(tdot(hidden, cot_low))

    d_attn = transposed_product(d_mid_low, w_out).astype(bf16)
    d_attn = split_heads(d_attn, q_heads).reshape(kv_heads, group, rows, HEAD_SIZE)
    grad_out = rep_sum_rows(tdot(attn_flat, d_mid_low))
    logsum = top + jnp.log(total)
    again = jnp.where(mask, jnp.exp(scores_of() - logsum), 0.0)
    grad_value = jnp.einsum(
        "kgqt,kgqd->ktd", again.astype(bf16), d_attn, preferred_element_type=f32
    )
    d_probs = jnp.einsum("kgqd,ktd->kgqt", d_attn, value_low, preferred_element_type=f32)
    delta = jnp.sum(d_attn.astype(f32) * attn.astype(f32), axis=-1, keepdims=True)
    d_score = (again * (d_probs - delta) * scale).astype(bf16)
    grad_qlow = jnp.einsum("kgqt,ktd->kgqd", d_score, key_low, preferred_element_type=f32)
    grad_klow = jnp.einsum("kgqt,kgqd->ktd", d_score, query_low, preferred_element_type=f32)
    d_query_norm = rotate(grad_qlow.reshape(q_heads, rows, HEAD_SIZE), cosine, -sine)
    d_key_norm = rotate(grad_klow, cosine, -sine)
    d_query = weighted_norm_reverse(query, inv_query, d_query_norm * gain_q)
    d_key = weighted_norm_reverse(key, inv_key, d_key_norm * gain_k)
    grad_gain_q = jnp.sum(d_query_norm * query * inv_query, axis=(0, 1))
    grad_gain_k = jnp.sum(d_key_norm * key * inv_key, axis=(0, 1))
    d_projected = jnp.concatenate(
        [join_heads(d_query), join_heads(d_key), join_heads(grad_value)], axis=1
    ).astype(bf16)
    weighted_in = lax.psum_scatter(
        transposed_product(d_projected, qkv_cols).astype(bf16),
        "fsdp",
        scatter_dimension=0,
        tiled=True,
    ).astype(f32)
    grad_tokens = d_mid + weighted_norm_reverse(tokens, inv_in, weighted_in)
    gain_sums = jnp.stack([grad_gain_q, grad_gain_k]).reshape(2, members, -1).transpose(1, 0, 2)
    gain_sums = jnp.pad(
        gain_sums, ((0, 0), (0, 14), (0, q_cols + 2 * kv_cols - gain_sums.shape[2]))
    )
    raw_qkv, gain_sums = rep_sum_columns(tdot(unit_in, d_projected), members, gain_sums)
    raw_qkv = raw_qkv.transpose(1, 0, 2)
    raw_qkv = jnp.concatenate(
        [
            raw_qkv[:, :, :q_cols].reshape(shard, q_all),
            raw_qkv[:, :, q_cols : q_cols + kv_cols].reshape(shard, kv_all),
            raw_qkv[:, :, q_cols + kv_cols :].reshape(shard, kv_all),
        ],
        axis=1,
    ).astype(f32)
    grad_g_attn = jnp.sum(w_qkv.astype(f32) * raw_qkv, axis=1)
    grad_g_ffn = jnp.sum(w_gate_up.astype(f32) * grad_gu, axis=1)
    gain_sums = gain_sums[:2, : g_query.shape[0]]
    return (
        output,
        grad_tokens,
        raw_qkv * g_attn_col,
        grad_out,
        grad_gu * g_ffn_col,
        grad_down,
        grad_g_attn,
        gain_sums[0],
        gain_sums[1],
        grad_g_ffn,
    )


def solution(mesh):
    copies, members = mesh.shape["rep"], mesh.shape["fsdp"]
    splits = KEY_VALUE_HEADS % members == 0 and HEAD_SIZE % copies == 0
    body = split_columns_body if splits else gathered_weights_body
    placed = (
        P(("rep", "fsdp"), None),
        P(),
        P(("rep", "fsdp"), None),
        P("fsdp", None),
        P("fsdp", None),
        P("fsdp", None),
        P("fsdp", None),
        P("fsdp"),
        P("fsdp"),
        P("fsdp"),
        P("fsdp"),
    )
    return jax.shard_map(
        body,
        mesh=mesh,
        in_specs=placed,
        out_specs=(
            P(("rep", "fsdp"), None),
            P(("rep", "fsdp"), None),
            P("fsdp", None),
            P("fsdp", None),
            P("fsdp", None),
            P("fsdp", None),
            P("fsdp"),
            P("fsdp"),
            P("fsdp"),
            P("fsdp"),
        ),
        check_vma=False,
    )
```
